512 devices in a mesh: wide: 64 (over y, x, core), narrow: 8 (over z).
Axes of the slice: x: 4, y: 8, z: 8, core: 2. Of those that a mesh axis runs over, the one named last changes fastest.
Arguments:
- matrix_slab: float32 [16, 4194304], P(None, ('wide', 'narrow')), may hold values from -6 to 6
- row_signs: int32 [4194304], P(('wide', 'narrow')), may hold values from -1 to 1, as said below
- sample_rows: int32 [524288], P(('wide', 'narrow')), may hold values from 0 to 7, as said below
Outputs:
- sketch: float32 [16, 524288], P(None, ('wide', 'narrow'))
- sketch_gram: float32 [16, 16], replicated
The draws below stay inside these ranges and needn't reach their ends.
Inputs may be any that keep to these rules, and one draw needn't show every extreme that they name: `row_signs`: each entry is +1 or -1. `sample_rows`: entry k is the offset of the k-th sampled row inside the run of 8 rows that starts at k * 8.
All inputs are finite; a program needn't handle non-finite values.
Results may differ from the reference program's by a relative error of at most 0.00013.
Values sent between devices are 32-bit elements; how exact they have to be, the bound alone decides.
A program may use at most 64 MiB of HBM per device.

```python
import math
import jax
import jax.numpy as jnp
from jax import lax

COLS = 16
R_DEV = 8192
S_DEV = 1024
ROWS = 4194304
SAMPLES = 524288


def draw_row_signs(key, part):
    picks = jax.random.randint(jax.random.fold_in(key, 11), (ROWS,), 0, 2)
    return (2 * picks - 1).astype(jnp.int32)


def draw_sample_rows(key, part):
    run_length = R_DEV // S_DEV
    offsets = jax.random.randint(jax.random.fold_in(key, 23), (SAMPLES,), 0, run_length)
    offsets = offsets.at[0].set(run_length - 1)
    offsets = offsets.at[1].set(0)
    return offsets.astype(jnp.int32)


def level_of(rng, shape, shards, least, high):
    factor_of, own = 1.0, jax.random.fold_in(rng, 6)
    for dim, shards_of in shards:
        steps = jnp.exp(jax.random.uniform(jax.random.fold_in(own, dim), (shards_of,), jnp.float32, least / len(shards), high / len(shards)))
        factor_of = factor_of * jnp.repeat(steps, shape[dim] // shards_of).reshape([-1 if axis == dim else 1 for axis in range(len(shape))])
    return factor_of


def centred(stream_key, extent, deviation, limit, cuts=(), kind=jnp.bfloat16):
    array = deviation * jax.random.normal(stream_key, extent, jnp.float32)
    if cuts:
        array = array * level_of(stream_key, extent, cuts, -0.22, 0.18)
    return jnp.clip(array, -limit, limit).astype(kind)


def setup_inputs(seed: int = 0) -> dict:
    seeds = jax.random.split(jax.random.key(seed), 4)
    return {
        "matrix_slab": centred(seeds[0], (COLS, ROWS), 1.0, 6.0, ((1, 512),), jnp.float32),
        "row_signs": draw_row_signs(jax.random.fold_in(seeds[3], 71), 0),
        "sample_rows": draw_sample_rows(jax.random.fold_in(seeds[3], 71), 0),
    }


def reference(matrix_slab, row_signs, sample_rows):
    values = matrix_slab * row_signs.astype(jnp.float32)[None, :]
    columns = values.shape[0]
    row_total = values.shape[1]
    stride_len = 1
    for section in range(row_total.bit_length() - 1):
        shaped = values.reshape(columns, row_total // (2 * stride_len), 2, stride_len)
        first_half = shaped[:, :, 0, :]
        second_half = shaped[:, :, 1, :]
        values = jnp.stack([first_half + second_half, first_half - second_half], axis=2).reshape(columns, row_total)
        stride_len = stride_len * 2
    values = values * jnp.float32(1.0 / math.sqrt(ROWS))
    run_length = R_DEV // S_DEV
    full_index = (jnp.arange(SAMPLES, dtype=jnp.int32) * run_length + sample_rows.astype(jnp.int32)).astype(jnp.int32)
    sketch = jnp.take(values, full_index, axis=1)
    sketch_gram = jnp.dot(sketch, sketch.T, precision=lax.Precision.HIGHEST, preferred_element_type=jnp.float32) / jnp.float32(SAMPLES)
    return (sketch, sketch_gram)
```

```python
import functools
import math

import jax
import jax.numpy as jnp
from jax import lax
from jax.experimental import pallas as pl
from jax.experimental.pallas import tpu as pltpu
from jax.sharding import PartitionSpec as P

MESH = pl.DeviceIdType.MESH
F32, BF16 = jnp.float32, jnp.bfloat16


def parity_sign(a, b, bits):
    common = a & b
    parity = jnp.zeros_like(common)
    for bit in range(bits):
        parity = parity ^ (common >> bit & 1)
    return (1 - 2 * parity).astype(F32)


def butterfly(tiles):
    tiles, step = list(tiles), 1
    while step < len(tiles):
        for i in range(len(tiles)):
            if not i & step:
                a, b = tiles[i], tiles[i + step]
                tiles[i], tiles[i + step] = a + b, a - b
        step *= 2
    return tiles


def parts(value, axis):
    high = value.astype(BF16)
    low = (value - high.astype(F32)).astype(BF16)
    return jnp.concatenate([high, low], axis=axis)


def kernel(
    nw, nz, scale, gram_scale,
    x_ref, sign_ref, rows_ref, sketch_ref, gram_ref,
    own, tiles, pick_own, pick_tiles, mixed, slabs, pick_z, picks,
    chosen, back, turn, ret, rec, gram_own, gram_w, gram_zown, gram_z,
    sem_w, sem_z, sem_p, sem_b, sem_g, sem_c,
):
    w, z = lax.axis_index("wide"), lax.axis_index("narrow")
    barrier = pltpu.get_barrier_semaphore()

    def each_wide(body):
        def step(i, carry):
            body(lax.rem(w + i, nw))
            return carry

        lax.fori_loop(1, nw, step, 0)

    def each_narrow(body):
        for i in range(1, nz):
            body(lax.rem(z + i, nz))

    each_wide(lambda p: pl.semaphore_signal(barrier, inc=1, device_id=(p, z), device_id_type=MESH))
    each_narrow(lambda p: pl.semaphore_signal(barrier, inc=1, device_id=(w, p), device_id_type=MESH))

    def to_wide(src, dst, sems, p):
        pltpu.make_async_remote_copy(
            src, dst, sems.at[0], sems.at[1], device_id=(p, z), device_id_type=MESH
        ).start()

    def to_narrow(src, dst, sems, p):
        pltpu.make_async_remote_copy(
            src, dst, sems.at[0], sems.at[1], device_id=(w, p), device_id_type=MESH
        ).start()

    def await_all(ref, sem):
        pltpu.make_async_copy(ref, ref, sem).wait()

    lane_i = lax.broadcasted_iota(jnp.int32, (128, 128), 1)
    row_i = lax.broadcasted_iota(jnp.int32, (128, 128), 0)
    lane_table = parity_sign(lane_i, row_i, 7).astype(BF16)
    lane_table = jnp.concatenate([lane_table, lane_table], axis=0)
    wide_table = jnp.where(lane_i // nw == row_i // nw, parity_sign(lane_i, row_i, 6), 0.0).astype(BF16)
    wide_table = jnp.concatenate([wide_table, wide_table], axis=0)

    offsets = rows_ref[...].astype(F32)
    for t in range(8):
        pick_own[t] = offsets[t : t + 1]

    def local(h):
        cols = slice(8 * h, 8 * h + 8)
        for g in range(8):
            part = []
            for i in range(8):
                t = g * 8 + i
                sign = sign_ref[t : t + 1, :].astype(F32)
                part.append(x_ref[cols, 128 * t : 128 * t + 128] * sign)
            for i, tile in enumerate(butterfly(part)):
                own[h, pl.ds(8 * (g * 8 + i), 8), :] = tile
        for g in range(8):
            part = butterfly([own[h, pl.ds(8 * (i * 8 + g), 8), :] for i in range(8)])
            value = jnp.dot(
                parts(jnp.concatenate(part, axis=0), 1), lane_table, preferred_element_type=F32
            )
            for i in range(8):
                own[h, pl.ds(8 * (i * 8 + g), 8), :] = value[8 * i : 8 * i + 8]

    def send_half(h):
        mine = pl.ds(pl.multiple_of(w * 8, 8), 8)

        def send(p):
            to_wide(own.at[h, pl.ds(pl.multiple_of(p * 8, 8), 8)], tiles.at[h, mine], sem_w.at[h], p)

        each_wide(send)
        tiles[h, mine, :] = own[h, mine, :]

    local(0)
    pl.semaphore_wait(barrier, nw - 1 + nz - 1)
    each_wide(lambda p: to_wide(pick_own.at[lax.div(p, 8)], pick_tiles.at[w], sem_p, p))
    pick_tiles[w] = pick_own[lax.div(w, 8)]
    send_half(0)
    local(1)
    send_half(1)

    await_all(pick_tiles.at[pl.ds(0, nw - 1)], sem_p.at[1])
    gathered = pick_tiles[...].reshape(nw, 128).astype(BF16)
    gathered = jnp.concatenate([gathered, gathered], axis=0)
    first = lax.rem(w, 8) * 16
    choose = (lane_i[:16] == row_i[:16] + first).astype(BF16)
    by_run = lax.dot_general(
        choose, gathered, (((1,), (1,)), ((), ())), preferred_element_type=F32
    )
    for k in range(8):
        pick_z[k] = by_run[2 * k : 2 * k + 2]
    each_narrow(lambda p: to_narrow(pick_z.at[p], picks.at[z], sem_c, p))
    picks[z] = pick_z[z]

    for h in range(2):
        await_all(tiles.at[h, pl.ds(0, 8 * (nw - 1))], sem_w.at[h, 1])
        for p in range(4):
            value = jnp.concatenate(
                [tiles[h, pl.ds(4 * c + p, nw, stride=8), :] for c in range(2)], axis=0
            )
            value = jnp.dot(parts(value.T, 1), wide_table, preferred_element_type=F32)
            for k in range(8):
                mixed[h, k, 16 * p : 16 * p + 16, :] = value[16 * k : 16 * k + 16]
        each_narrow(lambda p: to_narrow(mixed.at[h, p], slabs.at[h, z], sem_z.at[h], p))
        slabs[h, z] = mixed[h, z]

    await_all(picks.at[pl.ds(0, nz - 1)], sem_c.at[1])
    place = lax.broadcasted_iota(jnp.int32, (8, 128), 0).astype(F32)
    for h in range(2):
        await_all(slabs.at[h, pl.ds(0, nz - 1)], sem_z.at[h, 1])
        for k in range(2):
            masks = [picks[d, k : k + 1, :] == place for d in range(nz)]
            for p in range(4):
                at = 16 * p + 8 * k
                out = butterfly([slabs[h, s, at : at + 8, :] for s in range(nz)])
                for d in range(nz):
                    one = jnp.sum(jnp.where(masks[d], out[d], 0.0), axis=0, keepdims=True)
                    row = 8 * k + 4 * h + p
                    chosen[d, row : row + 1, :] = one * scale

    each_narrow(lambda p: to_narrow(chosen.at[p], back.at[z], sem_b, p))
    back[z] = chosen[z]

    lane = lane_i[:8]
    sub = row_i[:8]
    terms = []
    for d in range(nz):
        one, two = chosen[d, 0:8, :], chosen[d, 8:16, :]
        even = jnp.where(lane < 64, one, pltpu.roll(two, 64, 1))
        odd = jnp.where(lane < 64, pltpu.roll(one, 64, 1), two)
        top = jnp.where(sub < 4, even, pltpu.roll(odd, 4, 0))
        low = jnp.where(sub < 4, pltpu.roll(even, 4, 0), odd)
        terms.append(jnp.concatenate([top, low], axis=0))
    columns = jnp.concatenate(terms, axis=1)
    wide_gram = lax.dot_general(
        columns, jnp.concatenate([columns] * 8, axis=0), (((1,), (1,)), ((), ())),
        precision=lax.Precision.HIGHEST, preferred_element_type=F32,
    )
    diagonal = lane // 16 == sub
    for a in range(2):
        gram_own[0, a : a + 1, :] = jnp.sum(
            jnp.where(diagonal, wide_gram[8 * a : 8 * a + 8], 0.0), axis=0, keepdims=True
        )
    each_wide(lambda p: to_wide(gram_own.at[0], gram_w.at[w], sem_g.at[0], p))
    gram_w[w] = gram_own[0]

    await_all(back.at[pl.ds(0, nz - 1)], sem_b.at[1])
    for s in range(nz):
        for k in range(2):
            turn[pl.ds(2 * s + k, 8, stride=16), :] = back[s, 8 * k : 8 * k + 8, :]
    turned = turn[...].T
    ret[:, 0, :] = turned[:nw]
    ret[:, 1, :] = turned[nw:]
    each_wide(lambda p: to_wide(ret.at[p], rec.at[w], sem_p.at[pl.ds(2, 2)], p))
    rec[w] = ret[w]

    await_all(gram_w.at[pl.ds(0, nw - 1)], sem_g.at[0, 1])
    gram_zown[0] = jnp.sum(gram_w[...], axis=0)
    each_narrow(lambda p: to_narrow(gram_zown.at[0], gram_z.at[z], sem_g.at[1], p))
    gram_z[z] = gram_zown[0]

    await_all(rec.at[pl.ds(0, nw - 1)], sem_p.at[3])
    group = lane // 16
    for t in range(8):
        for c in range(2):
            value = rec[8 * t : 8 * t + 8, c, :]
            for bit in (1, 2, 4):
                down = pltpu.roll(pltpu.roll(value, 8 - bit, 0), 16 * bit, 1)
                up = pltpu.roll(pltpu.roll(value, bit, 0), 128 - 16 * bit, 1)
                upper, right = (sub & bit) != 0, (group & bit) != 0
                value = jnp.where(upper == right, value, jnp.where(right, down, up))
            for e in range(2):
                sketch_ref[8 * e + 4 * c : 8 * e + 4 * c + 4, 128 * t : 128 * t + 128] = value[4 * e : 4 * e + 4]

    await_all(gram_z.at[pl.ds(0, nz - 1)], sem_g.at[1, 1])
    gram_ref[...] = jnp.sum(gram_z[...], axis=0) * gram_scale

    for h in range(2):
        await_all(tiles.at[h, pl.ds(0, 8 * (nw - 1))], sem_w.at[h, 0])
        await_all(slabs.at[h, pl.ds(0, nz - 1)], sem_z.at[h, 0])
    await_all(pick_tiles.at[pl.ds(0, nw - 1)], sem_p.at[0])
    await_all(rec.at[pl.ds(0, nw - 1)], sem_p.at[2])
    await_all(picks.at[pl.ds(0, nz - 1)], sem_c.at[0])
    await_all(back.at[pl.ds(0, nz - 1)], sem_b.at[0])
    await_all(gram_w.at[pl.ds(0, nw - 1)], sem_g.at[0, 0])
    await_all(gram_z.at[pl.ds(0, nz - 1)], sem_g.at[1, 0])


def solution(mesh):
    nw, nz = mesh.shape["wide"], mesh.shape["narrow"]

    def shards(matrix_slab, row_signs, sample_rows):
        cols, rows = matrix_slab.shape
        samples = sample_rows.shape[0]
        dma = pltpu.SemaphoreType.DMA
        sketch, gram = pl.pallas_call(
            functools.partial(
                kernel, nw, nz, 1.0 / math.sqrt(rows * nw * nz), 1.0 / (samples * nw * nz)
            ),
            out_shape=(
                jax.ShapeDtypeStruct((cols, samples), F32),
                jax.ShapeDtypeStruct((2, 128), F32),
            ),
            in_specs=[pl.BlockSpec(memory_space=pltpu.VMEM)] * 3,
            out_specs=[pl.BlockSpec(memory_space=pltpu.VMEM)] * 2,
            scratch_shapes=[
                pltpu.VMEM((2, 8 * nw, 128), F32),
                pltpu.VMEM((2, 8 * nw, 128), F32),
                pltpu.VMEM((8, 1, 128), F32),
                pltpu.VMEM((nw, 1, 128), F32),
                pltpu.VMEM((2, nz, 64, 128), F32),
                pltpu.VMEM((2, nz, 64, 128), F32),
                pltpu.VMEM((nz, 2, 128), F32),
                pltpu.VMEM((nz, 2, 128), F32),
                pltpu.VMEM((nz, 16, 128), F32),
                pltpu.VMEM((nz, 16, 128), F32),
                pltpu.VMEM((128, 128), F32),
                pltpu.VMEM((nw, 2, 128), F32),
                pltpu.VMEM((nw, 2, 128), F32),
                pltpu.VMEM((1, 2, 128), F32),
                pltpu.VMEM((nw, 2, 128), F32),
                pltpu.VMEM((1, 2, 128), F32),
                pltpu.VMEM((nz, 2, 128), F32),
                dma((2, 2)),
                dma((2, 2)),
                dma((4,)),
                dma((2,)),
                dma((2, 2)),
                dma((2,)),
            ],
            compiler_params=pltpu.CompilerParams(
                collective_id=0, has_side_effects=True, vmem_limit_bytes=32 << 20
            ),
            name="hadamard_sketch",
        )(matrix_slab, row_signs.reshape(-1, 128), sample_rows.reshape(-1, 128))
        return sketch, gram.reshape(cols, cols)

    in_specs = (P(None, ("wide", "narrow")), P(("wide", "narrow")), P(("wide", "narrow")))
    out_specs = (P(None, ("wide", "narrow")), P())
    return jax.shard_map(shards, mesh=mesh, in_specs=in_specs, out_specs=out_specs, check_vma=False)
```

```python
import functools
import math

import jax
import jax.numpy as jnp
from jax import lax
from jax.experimental import pallas as pl
from jax.experimental.pallas import tpu as pltpu
from jax.sharding import PartitionSpec as P

MESH = pl.DeviceIdType.MESH
F32, BF16 = jnp.float32, jnp.bfloat16


def parity_sign(a, b, bits):
    common = a & b
    parity = jnp.zeros_like(common)
    for bit in range(bits):
        parity = parity ^ (common >> bit & 1)
    return (1 - 2 * parity).astype(F32)


def butterfly(tiles):
    tiles, step = list(tiles), 1
    while step < len(tiles):
        for i in range(len(tiles)):
            if not i & step:
                a, b = tiles[i], tiles[i + step]
                tiles[i], tiles[i + step] = a + b, a - b
        step *= 2
    return tiles


def parts(value, axis):
    high = value.astype(BF16)
    low = (value - high.astype(F32)).astype(BF16)
    return jnp.concatenate([high, low], axis=axis)


def kernel(
    nw, nz, scale, gram_scale,
    x_hbm, sign_hbm, rows_hbm, sketch_ref, gram_ref, x_ref, sign_ref, rows_ref,
    own, tiles, pick_own, pick_tiles, mixed, slabs, pick_z, picks,
    chosen, back, turn, ret, rec, gram_own, gram_w, gram_zown, gram_z,
    sem_in, sem_w, sem_z, sem_p, sem_b, sem_g, sem_c,
):
    w, z = lax.axis_index("wide"), lax.axis_index("narrow")
    barrier = pltpu.get_barrier_semaphore()

    inputs = [
        pltpu.make_async_copy(x_hbm.at[pl.ds(8 * h, 8)], x_ref.at[h], sem_in.at[h]) for h in range(2)
    ]
    inputs.append(pltpu.make_async_copy(sign_hbm, sign_ref, sem_in.at[2]))
    inputs.append(pltpu.make_async_copy(rows_hbm, rows_ref, sem_in.at[3]))
    for i in (0, 2, 1, 3):
        inputs[i].start()

    y, j = lax.div(w, 8), lax.rem(w, 8)

    def each_wide(body):
        def step(i, carry):
            k = lax.div(i, 8)
            half = lax.div(k + 1, 2)
            along = jnp.where(lax.rem(k, 2) == 1, 4 - half, 4 + half)
            body(lax.rem(y + along, 8) * 8 + lax.rem(j + 1 + lax.rem(i, 8), 8))
            return carry

        lax.fori_loop(0, nw - 1, step, 0)

    def each_narrow(body):
        for i in (4, 3, 5, 2, 6, 1, 7):
            body(lax.rem(z + i, nz))

    each_narrow(lambda p: pl.semaphore_signal(barrier, inc=1, device_id=(w, p), device_id_type=MESH))
    each_wide(lambda p: pl.semaphore_signal(barrier, inc=1, device_id=(p, z), device_id_type=MESH))

    def to_wide(src, dst, sems, p):
        pltpu.make_async_remote_copy(
            src, dst, sems.at[0], sems.at[1], device_id=(p, z), device_id_type=MESH
        ).start()

    def to_narrow(src, dst, sems, p):
        pltpu.make_async_remote_copy(
            src, dst, sems.at[0], sems.at[1], device_id=(w, p), device_id_type=MESH
        ).start()

    def await_all(ref, sem):
        pltpu.make_async_copy(ref, ref, sem).wait()

    lane_i = lax.broadcasted_iota(jnp.int32, (128, 128), 1)
    row_i = lax.broadcasted_iota(jnp.int32, (128, 128), 0)
    lane_table = parity_sign(lane_i, row_i, 7).astype(BF16)
    lane_table = jnp.concatenate([lane_table, lane_table], axis=0)
    wide_table = jnp.where(lane_i // nw == row_i // nw, parity_sign(lane_i, row_i, 6), 0.0).astype(BF16)
    wide_table = jnp.concatenate([wide_table, wide_table], axis=0)

    def local(h):
        for g in range(8):
            part = []
            for i in range(8):
                t = g * 8 + i
                sign = sign_ref[t : t + 1, :].astype(F32)
                part.append(x_ref[h, :, 128 * t : 128 * t + 128] * sign)
            for i, tile in enumerate(butterfly(part)):
                own[h, pl.ds(8 * (g * 8 + i), 8), :] = tile
        for g in range(8):
            part = butterfly([own[h, pl.ds(8 * (i * 8 + g), 8), :] for i in range(8)])
            value = jnp.dot(
                parts(jnp.concatenate(part, axis=0), 1), lane_table, preferred_element_type=F32
            )
            for i in range(8):
                own[h, pl.ds(8 * (i * 8 + g), 8), :] = value[8 * i : 8 * i + 8]

    def send_half(h):
        mine = pl.ds(pl.multiple_of(w * 8, 8), 8)

        def send(p):
            to_wide(own.at[h, pl.ds(pl.multiple_of(p * 8, 8), 8)], tiles.at[h, mine], sem_w.at[h], p)

        each_wide(send)
        tiles[h, mine, :] = own[h, mine, :]

    inputs[2].wait()
    inputs[0].wait()
    local(0)
    pl.semaphore_wait(barrier, nw - 1 + nz - 1)
    send_half(0)
    inputs[1].wait()
    local(1)
    send_half(1)

    inputs[3].wait()
    offsets = rows_ref[...].astype(F32)
    for t in range(8):
        pick_own[t] = offsets[t : t + 1]
    each_wide(lambda p: to_wide(pick_own.at[lax.div(p, 8)], pick_tiles.at[w], sem_p, p))
    pick_tiles[w] = pick_own[lax.div(w, 8)]

    for h in range(2):
        await_all(tiles.at[h, pl.ds(0, 8 * (nw - 1))], sem_w.at[h, 1])
        for p in range(4):
            value = jnp.concatenate(
                [tiles[h, pl.ds(4 * c + p, nw, stride=8), :] for c in range(2)], axis=0
            )
            value = jnp.dot(parts(value.T, 1), wide_table, preferred_element_type=F32)
            for k in range(8):
                mixed[h, k, 16 * p : 16 * p + 16, :] = value[16 * k : 16 * k + 16]
        each_narrow(lambda p: to_narrow(mixed.at[h, p], slabs.at[h, z], sem_z.at[h], p))
        slabs[h, z] = mixed[h, z]

    await_all(pick_tiles.at[pl.ds(0, nw - 1)], sem_p.at[1])
    gathered = pick_tiles[...].reshape(nw, 128).astype(BF16)
    gathered = jnp.concatenate([gathered, gathered], axis=0)
    first = lax.rem(w, 8) * 16
    choose = (lane_i[:16] == row_i[:16] + first).astype(BF16)
    by_run = lax.dot_general(
        choose, gathered, (((1,), (1,)), ((), ())), preferred_element_type=F32
    )
    for k in range(8):
        pick_z[k] = by_run[2 * k : 2 * k + 2]
    each_narrow(lambda p: to_narrow(pick_z.at[p], picks.at[z], sem_c, p))
    picks[z] = pick_z[z]

    await_all(picks.at[pl.ds(0, nz - 1)], sem_c.at[1])
    place = lax.broadcasted_iota(jnp.int32, (8, 128), 0).astype(F32)
    for h in range(2):
        await_all(slabs.at[h, pl.ds(0, nz - 1)], sem_z.at[h, 1])
        for k in range(2):
            masks = [picks[d, k : k + 1, :] == place for d in range(nz)]
            for p in range(4):
                at = 16 * p + 8 * k
                out = butterfly([slabs[h, s, at : at + 8, :] for s in range(nz)])
                for d in range(nz):
                    one = jnp.sum(jnp.where(masks[d], out[d], 0.0), axis=0, keepdims=True)
                    row = 8 * k + 4 * h + p
                    chosen[d, row : row + 1, :] = one * scale

    each_narrow(lambda p: to_narrow(chosen.at[p], back.at[z], sem_b, p))
    back[z] = chosen[z]

    lane = lane_i[:8]
    sub = row_i[:8]
    terms = []
    for d in range(nz):
        one, two = chosen[d, 0:8, :], chosen[d, 8:16, :]
        even = jnp.where(lane < 64, one, pltpu.roll(two, 64, 1))
        odd = jnp.where(lane < 64, pltpu.roll(one, 64, 1), two)
        top = jnp.where(sub < 4, even, pltpu.roll(odd, 4, 0))
        low = jnp.where(sub < 4, pltpu.roll(even, 4, 0), odd)
        terms.append(jnp.concatenate([top, low], axis=0))
    columns = jnp.concatenate(terms, axis=1)
    wide_gram = lax.dot_general(
        columns, jnp.concatenate([columns] * 8, axis=0), (((1,), (1,)), ((), ())),
        precision=lax.Precision.HIGHEST, preferred_element_type=F32,
    )
    diagonal = lane // 16 == sub
    for a in range(2):
        gram_own[0, a : a + 1, :] = jnp.sum(
            jnp.where(diagonal, wide_gram[8 * a : 8 * a + 8], 0.0), axis=0, keepdims=True
        )
    each_wide(lambda p: to_wide(gram_own.at[0], gram_w.at[w], sem_g.at[0], p))
    gram_w[w] = gram_own[0]

    await_all(back.at[pl.ds(0, nz - 1)], sem_b.at[1])
    for s in range(nz):
        for k in range(2):
            turn[pl.ds(2 * s + k, 8, stride=16), :] = back[s, 8 * k : 8 * k + 8, :]
    turned = turn[...].T
    ret[:, 0, :] = turned[:nw]
    ret[:, 1, :] = turned[nw:]
    each_wide(lambda p: to_wide(ret.at[p], rec.at[w], sem_p.at[pl.ds(2, 2)], p))
    rec[w] = ret[w]

    await_all(gram_w.at[pl.ds(0, nw - 1)], sem_g.at[0, 1])
    gram_zown[0] = jnp.sum(gram_w[...], axis=0)
    each_narrow(lambda p: to_narrow(gram_zown.at[0], gram_z.at[z], sem_g.at[1], p))
    gram_z[z] = gram_zown[0]

    await_all(rec.at[pl.ds(0, nw - 1)], sem_p.at[3])
    group = lane // 16
    for t in range(8):
        for c in range(2):
            value = rec[8 * t : 8 * t + 8, c, :]
            for bit in (1, 2, 4):
                down = pltpu.roll(pltpu.roll(value, 8 - bit, 0), 16 * bit, 1)
                up = pltpu.roll(pltpu.roll(value, bit, 0), 128 - 16 * bit, 1)
                upper, right = (sub & bit) != 0, (group & bit) != 0
                value = jnp.where(upper == right, value, jnp.where(right, down, up))
            for e in range(2):
                sketch_ref[8 * e + 4 * c : 8 * e + 4 * c + 4, 128 * t : 128 * t + 128] = value[4 * e : 4 * e + 4]

    await_all(gram_z.at[pl.ds(0, nz - 1)], sem_g.at[1, 1])
    gram_ref[...] = jnp.sum(gram_z[...], axis=0) * gram_scale

    for h in range(2):
        await_all(tiles.at[h, pl.ds(0, 8 * (nw - 1))], sem_w.at[h, 0])
        await_all(slabs.at[h, pl.ds(0, nz - 1)], sem_z.at[h, 0])
    await_all(pick_tiles.at[pl.ds(0, nw - 1)], sem_p.at[0])
    await_all(rec.at[pl.ds(0, nw - 1)], sem_p.at[2])
    await_all(picks.at[pl.ds(0, nz - 1)], sem_c.at[0])
    await_all(back.at[pl.ds(0, nz - 1)], sem_b.at[0])
    await_all(gram_w.at[pl.ds(0, nw - 1)], sem_g.at[0, 0])
    await_all(gram_z.at[pl.ds(0, nz - 1)], sem_g.at[1, 0])


def solution(mesh):
    nw, nz = mesh.shape["wide"], mesh.shape["narrow"]

    def shards(matrix_slab, row_signs, sample_rows):
        cols, rows = matrix_slab.shape
        samples = sample_rows.shape[0]
        dma = pltpu.SemaphoreType.DMA
        sketch, gram = pl.pallas_call(
            functools.partial(
                kernel, nw, nz, 1.0 / math.sqrt(rows * nw * nz), 1.0 / (samples * nw * nz)
            ),
            out_shape=(
                jax.ShapeDtypeStruct((cols, samples), F32),
                jax.ShapeDtypeStruct((2, 128), F32),
            ),
            in_specs=[pl.BlockSpec(memory_space=pl.ANY)] * 3,
            out_specs=[pl.BlockSpec(memory_space=pltpu.VMEM)] * 2,
            scratch_shapes=[
                pltpu.VMEM((2, 8, 8192), F32),
                pltpu.VMEM((64, 128), jnp.int32),
                pltpu.VMEM((8, 128), jnp.int32),
                pltpu.VMEM((2, 8 * nw, 128), F32),
                pltpu.VMEM((2, 8 * nw, 128), F32),
                pltpu.VMEM((8, 1, 128), F32),
                pltpu.VMEM((nw, 1, 128), F32),
                pltpu.VMEM((2, nz, 64, 128), F32),
                pltpu.VMEM((2, nz, 64, 128), F32),
                pltpu.VMEM((nz, 2, 128), F32),
                pltpu.VMEM((nz, 2, 128), F32),
                pltpu.VMEM((nz, 16, 128), F32),
                pltpu.VMEM((nz, 16, 128), F32),
                pltpu.VMEM((128, 128), F32),
                pltpu.VMEM((nw, 2, 128), F32),
                pltpu.VMEM((nw, 2, 128), F32),
                pltpu.VMEM((1, 2, 128), F32),
                pltpu.VMEM((nw, 2, 128), F32),
                pltpu.VMEM((1, 2, 128), F32),
                pltpu.VMEM((nz, 2, 128), F32),
                dma((4,)),
                dma((2, 2)),
                dma((2, 2)),
                dma((4,)),
                dma((2,)),
                dma((2, 2)),
                dma((2,)),
            ],
            compiler_params=pltpu.CompilerParams(collective_id=0, has_side_effects=True),
            name="hadamard_sketch",
        )(matrix_slab, row_signs.reshape(-1, 128), sample_rows.reshape(-1, 128))
        return sketch, gram.reshape(cols, cols)

    in_specs = (P(None, ("wide", "narrow")), P(("wide", "narrow")), P(("wide", "narrow")))
    out_specs = (P(None, ("wide", "narrow")), P())
    return jax.shard_map(shards, mesh=mesh, in_specs=in_specs, out_specs=out_specs, check_vma=False)
```

```python
import functools
import math

import jax
import jax.numpy as jnp
from jax import lax
from jax.experimental import pallas as pl
from jax.experimental.pallas import tpu as pltpu
from jax.sharding import PartitionSpec as P

MESH = pl.DeviceIdType.MESH
F32, BF16 = jnp.float32, jnp.bfloat16


def parity_sign(a, b, bits):
    common = a & b
    parity = jnp.zeros_like(common)
    for bit in range(bits):
        parity = parity ^ (common >> bit & 1)
    return (1 - 2 * parity).astype(F32)


def butterfly(tiles):
    tiles, step = list(tiles), 1
    while step < len(tiles):
        for i in range(len(tiles)):
            if not i & step:
                a, b = tiles[i], tiles[i + step]
                tiles[i], tiles[i + step] = a + b, a - b
        step *= 2
    return tiles


def parts(value, axis):
    high = value.astype(BF16)
    low = (value - high.astype(F32)).astype(BF16)
    return jnp.concatenate([high, low], axis=axis)


def kernel(
    nw, nz, scale, gram_scale,
    x_hbm, sign_hbm, rows_hbm, sketch_ref, gram_ref, x_ref, sign_ref, rows_ref,
    own, tiles, pick_own, pick_tiles, mixed, slabs, pick_z, picks,
    chosen, back, turn, ret, rec, gram_own, gram_w, gram_zown, gram_z,
    sem_in, sem_w, sem_z, sem_p, sem_b, sem_g, sem_c,
):
    wide, narrow = lax.axis_index("wide"), lax.axis_index("narrow")
    w, z = lax.div(wide, 8) * 8 + narrow, lax.rem(wide, 8)

    def device(group, member):
        return (lax.div(group, 8) * 8 + member, lax.rem(group, 8))

    barrier = pltpu.get_barrier_semaphore()

    inputs = [
        pltpu.make_async_copy(x_hbm.at[pl.ds(8 * h, 8)], x_ref.at[h], sem_in.at[h]) for h in range(2)
    ]
    inputs.append(pltpu.make_async_copy(sign_hbm, sign_ref, sem_in.at[2]))
    inputs.append(pltpu.make_async_copy(rows_hbm, rows_ref, sem_in.at[3]))
    for i in (0, 2, 1, 3):
        inputs[i].start()

    y, j = lax.div(w, 8), lax.rem(w, 8)

    def each_wide(body):
        def step(i, carry):
            k = lax.div(i, 8)
            half = lax.div(k + 1, 2)
            along = jnp.where(lax.rem(k, 2) == 1, 4 - half, 4 + half)
            body(lax.rem(y + along, 8) * 8 + lax.rem(j + 1 + lax.rem(i, 8), 8))
            return carry

        lax.fori_loop(0, nw - 1, step, 0)

    def each_narrow(body):
        for i in (4, 3, 5, 2, 6, 1, 7):
            body(lax.rem(z + i, nz))

    each_narrow(lambda p: pl.semaphore_signal(barrier, inc=1, device_id=device(w, p), device_id_type=MESH))
    each_wide(lambda p: pl.semaphore_signal(barrier, inc=1, device_id=device(p, z), device_id_type=MESH))

    def to_wide(src, dst, sems, p):
        pltpu.make_async_remote_copy(
            src, dst, sems.at[0], sems.at[1], device_id=device(p, z), device_id_type=MESH
        ).start()

    def to_narrow(src, dst, sems, p):
        pltpu.make_async_remote_copy(
            src, dst, sems.at[0], sems.at[1], device_id=device(w, p), device_id_type=MESH
        ).start()

    def await_all(ref, sem):
        pltpu.make_async_copy(ref, ref, sem).wait()

    lane_i = lax.broadcasted_iota(jnp.int32, (128, 128), 1)
    row_i = lax.broadcasted_iota(jnp.int32, (128, 128), 0)
    lane_table = parity_sign(lane_i, row_i, 7).astype(BF16)
    lane_table = jnp.concatenate([lane_table, lane_table], axis=0)
    wide_table = jnp.where(lane_i // nw == row_i // nw, parity_sign(lane_i, row_i, 6), 0.0).astype(BF16)
    wide_table = jnp.concatenate([wide_table, wide_table], axis=0)

    def local(h):
        for g in range(8):
            part = []
            for i in range(8):
                t = g * 8 + i
                sign = sign_ref[t : t + 1, :].astype(F32)
                part.append(x_ref[h, :, 128 * t : 128 * t + 128] * sign)
            for i, tile in enumerate(butterfly(part)):
                own[h, pl.ds(8 * (g * 8 + i), 8), :] = tile
        for g in range(8):
            part = butterfly([own[h, pl.ds(8 * (i * 8 + g), 8), :] for i in range(8)])
            value = jnp.dot(
                parts(jnp.concatenate(part, axis=0), 1), lane_table, preferred_element_type=F32
            )
            for i in range(8):
                own[h, pl.ds(8 * (i * 8 + g), 8), :] = value[8 * i : 8 * i + 8]

    def send_half(h):
        mine = pl.ds(pl.multiple_of(w * 8, 8), 8)

        def send(p):
            to_wide(own.at[h, pl.ds(pl.multiple_of(p * 8, 8), 8)], tiles.at[h, mine], sem_w.at[h], p)

        each_wide(send)
        tiles[h, mine, :] = own[h, mine, :]

    inputs[2].wait()
    inputs[0].wait()
    local(0)
    pl.semaphore_wait(barrier, nw - 1 + nz - 1)
    send_half(0)
    inputs[1].wait()
    local(1)
    send_half(1)

    inputs[3].wait()
    offsets = rows_ref[...].astype(F32)
    for t in range(8):
        pick_own[t] = offsets[t : t + 1]
    each_wide(lambda p: to_wide(pick_own.at[lax.div(p, 8)], pick_tiles.at[w], sem_p, p))
    pick_tiles[w] = pick_own[lax.div(w, 8)]

    for h in range(2):
        await_all(tiles.at[h, pl.ds(0, 8 * (nw - 1))], sem_w.at[h, 1])
        for p in range(4):
            value = jnp.concatenate(
                [tiles[h, pl.ds(4 * c + p, nw, stride=8), :] for c in range(2)], axis=0
            )
            value = jnp.dot(parts(value.T, 1), wide_table, preferred_element_type=F32)
            for k in range(8):
                mixed[h, k, 16 * p : 16 * p + 16, :] = value[16 * k : 16 * k + 16]
        each_narrow(lambda p: to_narrow(mixed.at[h, p], slabs.at[h, z], sem_z.at[h], p))
        slabs[h, z] = mixed[h, z]

    await_all(pick_tiles.at[pl.ds(0, nw - 1)], sem_p.at[1])
    gathered = pick_tiles[...].reshape(nw, 128).astype(BF16)
    gathered = jnp.concatenate([gathered, gathered], axis=0)
    first = lax.rem(w, 8) * 16
    choose = (lane_i[:16] == row_i[:16] + first).astype(BF16)
    by_run = lax.dot_general(
        choose, gathered, (((1,), (1,)), ((), ())), preferred_element_type=F32
    )
    for k in range(8):
        pick_z[k] = by_run[2 * k : 2 * k + 2]
    each_narrow(lambda p: to_narrow(pick_z.at[p], picks.at[z], sem_c, p))
    picks[z] = pick_z[z]

    await_all(picks.at[pl.ds(0, nz - 1)], sem_c.at[1])
    place = lax.broadcasted_iota(jnp.int32, (8, 128), 0).astype(F32)
    for h in range(2):
        await_all(slabs.at[h, pl.ds(0, nz - 1)], sem_z.at[h, 1])
        for k in range(2):
            masks = [picks[d, k : k + 1, :] == place for d in range(nz)]
            for p in range(4):
                at = 16 * p + 8 * k
                out = butterfly([slabs[h, s, at : at + 8, :] for s in range(nz)])
                for d in range(nz):
                    one = jnp.sum(jnp.where(masks[d], out[d], 0.0), axis=0, keepdims=True)
                    row = 8 * k + 4 * h + p
                    chosen[d, row : row + 1, :] = one * scale

    each_narrow(lambda p: to_narrow(chosen.at[p], back.at[z], sem_b, p))
    back[z] = chosen[z]

    lane = lane_i[:8]
    sub = row_i[:8]
    terms = []
    for d in range(nz):
        one, two = chosen[d, 0:8, :], chosen[d, 8:16, :]
        even = jnp.where(lane < 64, one, pltpu.roll(two, 64, 1))
        odd = jnp.where(lane < 64, pltpu.roll(one, 64, 1), two)
        top = jnp.where(sub < 4, even, pltpu.roll(odd, 4, 0))
        low = jnp.where(sub < 4, pltpu.roll(even, 4, 0), odd)
        terms.append(jnp.concatenate([top, low], axis=0))
    columns = jnp.concatenate(terms, axis=1)
    wide_gram = lax.dot_general(
        columns, jnp.concatenate([columns] * 8, axis=0), (((1,), (1,)), ((), ())),
        precision=lax.Precision.HIGHEST, preferred_element_type=F32,
    )
    diagonal = lane // 16 == sub
    for a in range(2):
        gram_own[0, a : a + 1, :] = jnp.sum(
            jnp.where(diagonal, wide_gram[8 * a : 8 * a + 8], 0.0), axis=0, keepdims=True
        )
    each_wide(lambda p: to_wide(gram_own.at[0], gram_w.at[w], sem_g.at[0], p))
    gram_w[w] = gram_own[0]

    await_all(back.at[pl.ds(0, nz - 1)], sem_b.at[1])
    for s in range(nz):
        for k in range(2):
            turn[pl.ds(2 * s + k, 8, stride=16), :] = back[s, 8 * k : 8 * k + 8, :]
    turned = turn[...].T
    ret[:, 0, :] = turned[:nw]
    ret[:, 1, :] = turned[nw:]
    each_wide(lambda p: to_wide(ret.at[p], rec.at[w], sem_p.at[pl.ds(2, 2)], p))
    rec[w] = ret[w]

    await_all(gram_w.at[pl.ds(0, nw - 1)], sem_g.at[0, 1])
    gram_zown[0] = jnp.sum(gram_w[...], axis=0)
    each_narrow(lambda p: to_narrow(gram_zown.at[0], gram_z.at[z], sem_g.at[1], p))
    gram_z[z] = gram_zown[0]

    await_all(rec.at[pl.ds(0, nw - 1)], sem_p.at[3])
    group = lane // 16
    for t in range(8):
        for c in range(2):
            value = rec[8 * t : 8 * t + 8, c, :]
            for bit in (1, 2, 4):
                down = pltpu.roll(pltpu.roll(value, 8 - bit, 0), 16 * bit, 1)
                up = pltpu.roll(pltpu.roll(value, bit, 0), 128 - 16 * bit, 1)
                upper, right = (sub & bit) != 0, (group & bit) != 0
                value = jnp.where(upper == right, value, jnp.where(right, down, up))
            for e in range(2):
                sketch_ref[8 * e + 4 * c : 8 * e + 4 * c + 4, 128 * t : 128 * t + 128] = value[4 * e : 4 * e + 4]

    await_all(gram_z.at[pl.ds(0, nz - 1)], sem_g.at[1, 1])
    gram_ref[...] = jnp.sum(gram_z[...], axis=0) * gram_scale

    for h in range(2):
        await_all(tiles.at[h, pl.ds(0, 8 * (nw - 1))], sem_w.at[h, 0])
        await_all(slabs.at[h, pl.ds(0, nz - 1)], sem_z.at[h, 0])
    await_all(pick_tiles.at[pl.ds(0, nw - 1)], sem_p.at[0])
    await_all(rec.at[pl.ds(0, nw - 1)], sem_p.at[2])
    await_all(picks.at[pl.ds(0, nz - 1)], sem_c.at[0])
    await_all(back.at[pl.ds(0, nz - 1)], sem_b.at[0])
    await_all(gram_w.at[pl.ds(0, nw - 1)], sem_g.at[0, 0])
    await_all(gram_z.at[pl.ds(0, nz - 1)], sem_g.at[1, 0])


def solution(mesh):
    nw, nz = mesh.shape["wide"], mesh.shape["narrow"]

    def shards(matrix_slab, row_signs, sample_rows):
        cols, rows = matrix_slab.shape
        samples = sample_rows.shape[0]
        dma = pltpu.SemaphoreType.DMA
        sketch, gram = pl.pallas_call(
            functools.partial(
                kernel, nw, nz, 1.0 / math.sqrt(rows * nw * nz), 1.0 / (samples * nw * nz)
            ),
            out_shape=(
                jax.ShapeDtypeStruct((cols, samples), F32),
                jax.ShapeDtypeStruct((2, 128), F32),
            ),
            in_specs=[pl.BlockSpec(memory_space=pl.ANY)] * 3,
            out_specs=[pl.BlockSpec(memory_space=pltpu.VMEM)] * 2,
            scratch_shapes=[
                pltpu.VMEM((2, 8, 8192), F32),
                pltpu.VMEM((64, 128), jnp.int32),
                pltpu.VMEM((8, 128), jnp.int32),
                pltpu.VMEM((2, 8 * nw, 128), F32),
                pltpu.VMEM((2, 8 * nw, 128), F32),
                pltpu.VMEM((8, 1, 128), F32),
                pltpu.VMEM((nw, 1, 128), F32),
                pltpu.VMEM((2, nz, 64, 128), F32),
                pltpu.VMEM((2, nz, 64, 128), F32),
                pltpu.VMEM((nz, 2, 128), F32),
                pltpu.VMEM((nz, 2, 128), F32),
                pltpu.VMEM((nz, 16, 128), F32),
                pltpu.VMEM((nz, 16, 128), F32),
                pltpu.VMEM((128, 128), F32),
                pltpu.VMEM((nw, 2, 128), F32),
                pltpu.VMEM((nw, 2, 128), F32),
                pltpu.VMEM((1, 2, 128), F32),
                pltpu.VMEM((nw, 2, 128), F32),
                pltpu.VMEM((1, 2, 128), F32),
                pltpu.VMEM((nz, 2, 128), F32),
                dma((4,)),
                dma((2, 2)),
                dma((2, 2)),
                dma((4,)),
                dma((2,)),
                dma((2, 2)),
                dma((2,)),
            ],
            compiler_params=pltpu.CompilerParams(collective_id=0, has_side_effects=True),
            name="hadamard_sketch",
        )(matrix_slab, row_signs.reshape(-1, 128), sample_rows.reshape(-1, 128))
        return sketch, gram.reshape(cols, cols)

    in_specs = (P(None, ("wide", "narrow")), P(("wide", "narrow")), P(("wide", "narrow")))
    out_specs = (P(None, ("wide", "narrow")), P())
    return jax.shard_map(shards, mesh=mesh, in_specs=in_specs, out_specs=out_specs, check_vma=False)
```

```python
import functools
import math

import jax
import jax.numpy as jnp
from jax import lax
from jax.experimental import pallas as pl
from jax.experimental.pallas import tpu as pltpu
from jax.sharding import PartitionSpec as P

MESH = pl.DeviceIdType.MESH
F32, BF16 = jnp.float32, jnp.bfloat16


def parity_sign(a, b, bits):
    common = a & b
    parity = jnp.zeros_like(common)
    for bit in range(bits):
        parity = parity ^ (common >> bit & 1)
    return (1 - 2 * parity).astype(F32)


def butterfly(tiles):
    tiles, step = list(tiles), 1
    while step < len(tiles):
        for i in range(len(tiles)):
            if not i & step:
                a, b = tiles[i], tiles[i + step]
                tiles[i], tiles[i + step] = a + b, a - b
        step *= 2
    return tiles


def parts(value, axis):
    high = value.astype(BF16)
    low = (value - high.astype(F32)).astype(BF16)
    return jnp.concatenate([high, low], axis=axis)


def kernel(
    nw, nz, scale, gram_scale,
    x_hbm, sign_hbm, rows_hbm, samples_ref, gram_ref, x_ref, sign_ref, rows_ref,
    own, tiles, pick_own, pick_tiles, mixed, slabs, pick_z, picks,
    chosen, back, turn, ret, rec, gram_own, gram_w, gram_zown, gram_z,
    sem_in, sem_w, sem_z, sem_p, sem_b, sem_g, sem_c,
):
    wide, narrow = lax.axis_index("wide"), lax.axis_index("narrow")
    w, z = lax.div(wide, 8) * 8 + narrow, lax.rem(wide, 8)

    def device(group, member):
        return (lax.div(group, 8) * 8 + member, lax.rem(group, 8))

    barrier = pltpu.get_barrier_semaphore()

    inputs = [
        pltpu.make_async_copy(x_hbm.at[pl.ds(8 * h, 8)], x_ref.at[h], sem_in.at[h]) for h in range(2)
    ]
    inputs.append(pltpu.make_async_copy(sign_hbm, sign_ref, sem_in.at[2]))
    inputs.append(pltpu.make_async_copy(rows_hbm, rows_ref, sem_in.at[3]))
    for i in (0, 2, 1, 3):
        inputs[i].start()

    y, j = lax.div(w, 8), lax.rem(w, 8)

    def each_wide(body):
        def step(i, carry):
            k = lax.div(i, 8)
            half = lax.div(k + 1, 2)
            along = jnp.where(lax.rem(k, 2) == 1, 4 - half, 4 + half)
            body(lax.rem(y + along, 8) * 8 + lax.rem(j + 1 + lax.rem(i, 8), 8))
            return carry

        lax.fori_loop(0, nw - 1, step, 0)

    def each_narrow(body):
        for i in (4, 3, 5, 2, 6, 1, 7):
            body(lax.rem(z + i, nz))

    each_narrow(lambda p: pl.semaphore_signal(barrier, inc=1, device_id=device(w, p), device_id_type=MESH))
    each_wide(lambda p: pl.semaphore_signal(barrier, inc=1, device_id=device(p, z), device_id_type=MESH))

    def to_wide(src, dst, sems, p):
        pltpu.make_async_remote_copy(
            src, dst, sems.at[0], sems.at[1], device_id=device(p, z), device_id_type=MESH
        ).start()

    def to_narrow(src, dst, sems, p):
        pltpu.make_async_remote_copy(
            src, dst, sems.at[0], sems.at[1], device_id=device(w, p), device_id_type=MESH
        ).start()

    def await_all(ref, sem):
        pltpu.make_async_copy(ref, ref, sem).wait()

    lane_i = lax.broadcasted_iota(jnp.int32, (128, 128), 1)
    row_i = lax.broadcasted_iota(jnp.int32, (128, 128), 0)
    lane_table = parity_sign(lane_i, row_i, 7).astype(BF16)
    lane_table = jnp.concatenate([lane_table, lane_table], axis=0)
    def local(h):
        for g in range(8):
            part = []
            for i in range(8):
                t = g * 8 + i
                sign = sign_ref[t : t + 1, :].astype(F32)
                part.append(x_ref[h, :, 128 * t : 128 * t + 128] * sign)
            for i, tile in enumerate(butterfly(part)):
                own[h, pl.ds(8 * (g * 8 + i), 8), :] = tile
        for g in range(8):
            part = butterfly([own[h, pl.ds(8 * (i * 8 + g), 8), :] for i in range(8)])
            value = jnp.dot(
                parts(jnp.concatenate(part, axis=0), 1), lane_table, preferred_element_type=F32
            )
            for i in range(8):
                own[h, pl.ds(8 * (i * 8 + g), 8), :] = value[8 * i : 8 * i + 8]

    def send_half(h):
        mine = pl.ds(pl.multiple_of(w * 8, 8), 8)

        def send(p):
            to_wide(own.at[h, pl.ds(pl.multiple_of(p * 8, 8), 8)], tiles.at[h, mine], sem_w.at[h], p)

        each_wide(send)
        tiles[h, mine, :] = own[h, mine, :]

    inputs[2].wait()
    inputs[0].wait()
    local(0)
    pl.semaphore_wait(barrier, nw - 1 + nz - 1)
    send_half(0)
    inputs[1].wait()
    local(1)
    send_half(1)

    wide_table = jnp.where(lane_i // nw == row_i // nw, parity_sign(lane_i, row_i, 6), 0.0).astype(BF16)
    wide_table = jnp.concatenate([wide_table, wide_table], axis=0)

    inputs[3].wait()
    offsets = rows_ref[...].astype(F32)
    for t in range(8):
        pick_own[t] = offsets[t : t + 1]
    each_wide(lambda p: to_wide(pick_own.at[lax.div(p, 8)], pick_tiles.at[w], sem_p, p))
    pick_tiles[w] = pick_own[lax.div(w, 8)]

    for h in range(2):
        await_all(tiles.at[h, pl.ds(0, 8 * (nw - 1))], sem_w.at[h, 1])
        for p in range(4):
            value = jnp.concatenate(
                [tiles[h, pl.ds(4 * c + p, nw, stride=8), :] for c in range(2)], axis=0
            )
            value = jnp.dot(parts(value.T, 1), wide_table, preferred_element_type=F32)
            for k in range(8):
                mixed[h, k, 16 * p : 16 * p + 16, :] = value[16 * k : 16 * k + 16]
        each_narrow(lambda p: to_narrow(mixed.at[h, p], slabs.at[h, z], sem_z.at[h], p))
        slabs[h, z] = mixed[h, z]

    await_all(pick_tiles.at[pl.ds(0, nw - 1)], sem_p.at[1])
    gathered = pick_tiles[...].reshape(nw, 128).astype(BF16)
    gathered = jnp.concatenate([gathered, gathered], axis=0)
    first = lax.rem(w, 8) * 16
    choose = (lane_i[:16] == row_i[:16] + first).astype(BF16)
    by_run = lax.dot_general(
        choose, gathered, (((1,), (1,)), ((), ())), preferred_element_type=F32
    )
    for k in range(8):
        pick_z[k] = by_run[2 * k : 2 * k + 2]
    each_narrow(lambda p: to_narrow(pick_z.at[p], picks.at[z], sem_c, p))
    picks[z] = pick_z[z]

    await_all(picks.at[pl.ds(0, nz - 1)], sem_c.at[1])
    place = lax.broadcasted_iota(jnp.int32, (8, 128), 0).astype(F32)
    for h in range(2):
        await_all(slabs.at[h, pl.ds(0, nz - 1)], sem_z.at[h, 1])
        for k in range(2):
            masks = [picks[d, k : k + 1, :] == place for d in range(nz)]
            for p in range(4):
                at = 16 * p + 8 * k
                out = butterfly([slabs[h, s, at : at + 8, :] for s in range(nz)])
                for d in range(nz):
                    one = jnp.sum(jnp.where(masks[d], out[d], 0.0), axis=0, keepdims=True)
                    row = 8 * k + 4 * h + p
                    chosen[d, row : row + 1, :] = one * scale

    each_narrow(lambda p: to_narrow(chosen.at[p], back.at[z], sem_b, p))
    back[z] = chosen[z]

    lane = lane_i[:8]
    sub = row_i[:8]
    terms = []
    for d in range(nz):
        one, two = chosen[d, 0:8, :], chosen[d, 8:16, :]
        even = jnp.where(lane < 64, one, pltpu.roll(two, 64, 1))
        odd = jnp.where(lane < 64, pltpu.roll(one, 64, 1), two)
        top = jnp.where(sub < 4, even, pltpu.roll(odd, 4, 0))
        low = jnp.where(sub < 4, pltpu.roll(even, 4, 0), odd)
        terms.append(jnp.concatenate([top, low], axis=0))
    columns = jnp.concatenate(terms, axis=1)
    high = columns.astype(BF16)
    low = (columns - high.astype(F32)).astype(BF16)
    repeated = jnp.concatenate([jnp.concatenate([high, low, high], axis=1)] * 8, axis=0)
    wide_gram = lax.dot_general(
        jnp.concatenate([high, high, low], axis=1), repeated, (((1,), (1,)), ((), ())),
        preferred_element_type=F32,
    )
    diagonal = lane // 16 == sub
    for a in range(2):
        gram_own[0, a : a + 1, :] = jnp.sum(
            jnp.where(diagonal, wide_gram[8 * a : 8 * a + 8], 0.0), axis=0, keepdims=True
        )
    each_wide(lambda p: to_wide(gram_own.at[0], gram_w.at[w], sem_g.at[0], p))
    gram_w[w] = gram_own[0]

    await_all(back.at[pl.ds(0, nz - 1)], sem_b.at[1])
    for s in range(nz):
        for k in range(2):
            turn[pl.ds(2 * s + k, 8, stride=16), :] = back[s, 8 * k : 8 * k + 8, :]
    turned = turn[...].T
    ret[:, 0, :] = turned[:nw]
    ret[:, 1, :] = turned[nw:]
    each_wide(lambda p: to_wide(ret.at[p], rec.at[w], sem_p.at[pl.ds(2, 2)], p))
    rec[w] = ret[w]

    await_all(gram_w.at[pl.ds(0, nw - 1)], sem_g.at[0, 1])
    gram_zown[0] = jnp.sum(gram_w[...], axis=0)
    each_narrow(lambda p: to_narrow(gram_zown.at[0], gram_z.at[z], sem_g.at[1], p))
    gram_z[z] = gram_zown[0]

    await_all(rec.at[pl.ds(0, nw - 1)], sem_p.at[3])
    samples_ref[...] = rec[...]
    await_all(gram_z.at[pl.ds(0, nz - 1)], sem_g.at[1, 1])
    gram_ref[...] = jnp.sum(gram_z[...], axis=0) * gram_scale

    for h in range(2):
        await_all(tiles.at[h, pl.ds(0, 8 * (nw - 1))], sem_w.at[h, 0])
        await_all(slabs.at[h, pl.ds(0, nz - 1)], sem_z.at[h, 0])
    await_all(pick_tiles.at[pl.ds(0, nw - 1)], sem_p.at[0])
    await_all(rec.at[pl.ds(0, nw - 1)], sem_p.at[2])
    await_all(picks.at[pl.ds(0, nz - 1)], sem_c.at[0])
    await_all(back.at[pl.ds(0, nz - 1)], sem_b.at[0])
    await_all(gram_w.at[pl.ds(0, nw - 1)], sem_g.at[0, 0])
    await_all(gram_z.at[pl.ds(0, nz - 1)], sem_g.at[1, 0])


def arrange(samples_ref, total_ref, sketch_ref, gram_ref):
    lane = lax.broadcasted_iota(jnp.int32, (8, 128), 1)
    sub = lax.broadcasted_iota(jnp.int32, (8, 128), 0)
    group = lane // 16
    for t in range(8):
        for c in range(2):
            value = samples_ref[8 * t : 8 * t + 8, c, :]
            for bit in (1, 2, 4):
                down = pltpu.roll(pltpu.roll(value, 8 - bit, 0), 16 * bit, 1)
                up = pltpu.roll(pltpu.roll(value, bit, 0), 128 - 16 * bit, 1)
                upper, right = (sub & bit) != 0, (group & bit) != 0
                value = jnp.where(upper == right, value, jnp.where(right, down, up))
            for e in range(2):
                sketch_ref[8 * e + 4 * c : 8 * e + 4 * c + 4, 128 * t : 128 * t + 128] = value[4 * e : 4 * e + 4]

    for a in range(2):
        value = jnp.broadcast_to(total_ref[a : a + 1, :], (8, 128))
        for bit in (1, 2, 4):
            value = jnp.where((sub & bit) != 0, pltpu.roll(value, 128 - 16 * bit, 1), value)
        gram_ref[8 * a : 8 * a + 8, :] = value[:, :16]


def solution(mesh):
    nw, nz = mesh.shape["wide"], mesh.shape["narrow"]

    def shards(matrix_slab, row_signs, sample_rows):
        cols, rows = matrix_slab.shape
        samples = sample_rows.shape[0]
        dma = pltpu.SemaphoreType.DMA
        ready, total = pl.pallas_call(
            functools.partial(
                kernel, nw, nz, 1.0 / math.sqrt(rows * nw * nz), 1.0 / (samples * nw * nz)
            ),
            out_shape=(
                jax.ShapeDtypeStruct((nw, 2, 128), F32),
                jax.ShapeDtypeStruct((2, 128), F32),
            ),
            in_specs=[pl.BlockSpec(memory_space=pl.ANY)] * 3,
            out_specs=[pl.BlockSpec(memory_space=pltpu.VMEM)] * 2,
            scratch_shapes=[
                pltpu.VMEM((2, 8, 8192), F32),
                pltpu.VMEM((64, 128), jnp.int32),
                pltpu.VMEM((8, 128), jnp.int32),
                pltpu.VMEM((2, 8 * nw, 128), F32),
                pltpu.VMEM((2, 8 * nw, 128), F32),
                pltpu.VMEM((8, 1, 128), F32),
                pltpu.VMEM((nw, 1, 128), F32),
                pltpu.VMEM((2, nz, 64, 128), F32),
                pltpu.VMEM((2, nz, 64, 128), F32),
                pltpu.VMEM((nz, 2, 128), F32),
                pltpu.VMEM((nz, 2, 128), F32),
                pltpu.VMEM((nz, 16, 128), F32),
                pltpu.VMEM((nz, 16, 128), F32),
                pltpu.VMEM((128, 128), F32),
                pltpu.VMEM((nw, 2, 128), F32),
                pltpu.VMEM((nw, 2, 128), F32),
                pltpu.VMEM((1, 2, 128), F32),
                pltpu.VMEM((nw, 2, 128), F32),
                pltpu.VMEM((1, 2, 128), F32),
                pltpu.VMEM((nz, 2, 128), F32),
                dma((4,)),
                dma((2, 2)),
                dma((2, 2)),
                dma((4,)),
                dma((2,)),
                dma((2, 2)),
                dma((2,)),
            ],
            compiler_params=pltpu.CompilerParams(collective_id=0, has_side_effects=True),
            name="hadamard_sketch",
        )(matrix_slab, row_signs.reshape(-1, 128), sample_rows.reshape(-1, 128))
        return pl.pallas_call(
            arrange,
            out_shape=(
                jax.ShapeDtypeStruct((cols, samples), F32),
                jax.ShapeDtypeStruct((cols, cols), F32),
            ),
            in_specs=[pl.BlockSpec(memory_space=pltpu.VMEM)] * 2,
            out_specs=[pl.BlockSpec(memory_space=pltpu.VMEM)] * 2,
            name="arrange",
        )(ready, total)

    in_specs = (P(None, ("wide", "narrow")), P(("wide", "narrow")), P(("wide", "narrow")))
    out_specs = (P(None, ("wide", "narrow")), P())
    return jax.shard_map(shards, mesh=mesh, in_specs=in_specs, out_specs=out_specs, check_vma=False)
```

```python
import functools
import math

import jax
import jax.numpy as jnp
from jax import lax
from jax.experimental import pallas as pl
from jax.experimental.pallas import tpu as pltpu
from jax.sharding import PartitionSpec as P

MESH = pl.DeviceIdType.MESH
F32, BF16 = jnp.float32, jnp.bfloat16


def parity_sign(a, b, bits):
    common = a & b
    parity = jnp.zeros_like(common)
    for bit in range(bits):
        parity = parity ^ (common >> bit & 1)
    return (1 - 2 * parity).astype(F32)


def butterfly(tiles):
    tiles, step = list(tiles), 1
    while step < len(tiles):
        for i in range(len(tiles)):
            if not i & step:
                a, b = tiles[i], tiles[i + step]
                tiles[i], tiles[i + step] = a + b, a - b
        step *= 2
    return tiles


def parts(value, axis):
    high = value.astype(BF16)
    low = (value - high.astype(F32)).astype(BF16)
    return jnp.concatenate([high, low], axis=axis)


def kernel(
    nw, nz, scale, gram_scale,
    x_hbm, sign_hbm, rows_hbm, samples_ref, gram_ref, x_ref, sign_ref, rows_ref,
    own, tiles, pick_own, pick_tiles, mixed, slabs, pick_z, picks,
    chosen, back, turn, ret, rec, gram_own, gram_w, gram_zown, gram_z,
    late_own, late, sem_in, sem_w, sem_z, sem_p, sem_b, sem_g, sem_c,
):
    wide, narrow = lax.axis_index("wide"), lax.axis_index("narrow")
    w, z = lax.div(wide, 8) * 8 + narrow, lax.rem(wide, 8)

    def device(group, member):
        return (lax.div(group, 8) * 8 + member, lax.rem(group, 8))

    barrier = pltpu.get_barrier_semaphore()

    inputs = [
        pltpu.make_async_copy(x_hbm.at[pl.ds(8 * h, 8)], x_ref.at[h], sem_in.at[h]) for h in range(2)
    ]
    inputs.append(pltpu.make_async_copy(sign_hbm, sign_ref, sem_in.at[2]))
    inputs.append(pltpu.make_async_copy(rows_hbm, rows_ref, sem_in.at[3]))
    for i in (0, 2, 1, 3):
        inputs[i].start()

    y, j = lax.div(w, 8), lax.rem(w, 8)

    def each_wide(body):
        def step(i, carry):
            k = lax.div(i, 8)
            half = lax.div(k + 1, 2)
            along = jnp.where(lax.rem(k, 2) == 1, 4 - half, 4 + half)
            body(lax.rem(y + along, 8) * 8 + lax.rem(j + 1 + lax.rem(i, 8), 8))
            return carry

        lax.fori_loop(0, nw - 1, step, 0)

    def each_narrow(body):
        for i in (4, 3, 5, 2, 6, 1, 7):
            body(lax.rem(z + i, nz))

    each_narrow(lambda p: pl.semaphore_signal(barrier, inc=1, device_id=device(w, p), device_id_type=MESH))
    each_wide(lambda p: pl.semaphore_signal(barrier, inc=1, device_id=device(p, z), device_id_type=MESH))

    def to_wide(src, dst, sems, p):
        pltpu.make_async_remote_copy(
            src, dst, sems.at[0], sems.at[1], device_id=device(p, z), device_id_type=MESH
        ).start()

    def to_narrow(src, dst, sems, p):
        pltpu.make_async_remote_copy(
            src, dst, sems.at[0], sems.at[1], device_id=device(w, p), device_id_type=MESH
        ).start()

    def await_all(ref, sem):
        pltpu.make_async_copy(ref, ref, sem).wait()

    lane_i = lax.broadcasted_iota(jnp.int32, (128, 128), 1)
    row_i = lax.broadcasted_iota(jnp.int32, (128, 128), 0)
    lane_table = parity_sign(lane_i, row_i, 7).astype(BF16)
    lane_table = jnp.concatenate([lane_table, lane_table], axis=0)
    def local(h):
        for g in range(8):
            part = []
            for i in range(8):
                t = g * 8 + i
                sign = sign_ref[t : t + 1, :].astype(F32)
                part.append(x_ref[h, :, 128 * t : 128 * t + 128] * sign)
            for i, tile in enumerate(butterfly(part)):
                own[h, pl.ds(8 * (g * 8 + i), 8), :] = tile
        for g in range(8):
            part = butterfly([own[h, pl.ds(8 * (i * 8 + g), 8), :] for i in range(8)])
            value = jnp.dot(
                parts(jnp.concatenate(part, axis=0), 1), lane_table, preferred_element_type=F32
            )
            for i in range(8):
                t = i * 8 + g
                if h == 0:
                    own[h, pl.ds(8 * t, 8), :] = value[8 * i : 8 * i + 8]
                    continue
                for r in range(4):
                    at = 8 * i + 2 * r
                    late_own[r & 1, t, 2 * (r >> 1) : 2 * (r >> 1) + 2, :] = value[at : at + 2]

    def send_half():
        mine = pl.ds(pl.multiple_of(w * 8, 8), 8)

        def send(p):
            to_wide(own.at[0, pl.ds(pl.multiple_of(p * 8, 8), 8)], tiles.at[mine], sem_w.at[0], p)

        each_wide(send)
        tiles[mine, :] = own[0, mine, :]

    def send_quarter(q):
        each_wide(lambda p: to_wide(late_own.at[q, p], late.at[q, w], sem_w.at[1 + q], p))
        late[q, w] = late_own[q, w]

    inputs[2].wait()
    inputs[0].wait()
    local(0)
    pl.semaphore_wait(barrier, nw - 1 + nz - 1)
    send_half()
    inputs[1].wait()
    local(1)
    send_quarter(0)
    send_quarter(1)

    wide_table = jnp.where(lane_i // nw == row_i // nw, parity_sign(lane_i, row_i, 6), 0.0).astype(BF16)
    wide_table = jnp.concatenate([wide_table, wide_table], axis=0)

    inputs[3].wait()
    offsets = rows_ref[...].astype(F32)
    for t in range(8):
        pick_own[t] = offsets[t : t + 1]
    each_wide(lambda p: to_wide(pick_own.at[lax.div(p, 8)], pick_tiles.at[w], sem_p, p))
    pick_tiles[w] = pick_own[lax.div(w, 8)]

    def mix(h, p, halves):
        value = jnp.concatenate(halves, axis=0)
        value = jnp.dot(parts(value.T, 1), wide_table, preferred_element_type=F32)
        for k in range(8):
            mixed[h, k, 16 * p : 16 * p + 16, :] = value[16 * k : 16 * k + 16]

    await_all(tiles.at[pl.ds(0, 8 * (nw - 1))], sem_w.at[0, 1])
    for p in range(4):
        mix(0, p, [tiles[pl.ds(4 * a + p, nw, stride=8), :] for a in range(2)])
    each_narrow(lambda p: to_narrow(mixed.at[0, p], slabs.at[0, z], sem_z.at[0], p))
    slabs[0, z] = mixed[0, z]
    for q in range(2):
        await_all(late.at[q, pl.ds(0, nw - 1)], sem_w.at[1 + q, 1])
        for f in range(2):
            mix(1, 2 * q + f, [late[q, :, 2 * a + f, :] for a in range(2)])
        part = pl.ds(32 * q, 32)
        each_narrow(
            lambda p: to_narrow(mixed.at[1, p, part], slabs.at[1, z, part], sem_z.at[1], p)
        )
    slabs[1, z] = mixed[1, z]

    await_all(pick_tiles.at[pl.ds(0, nw - 1)], sem_p.at[1])
    gathered = pick_tiles[...].reshape(nw, 128).astype(BF16)
    gathered = jnp.concatenate([gathered, gathered], axis=0)
    first = lax.rem(w, 8) * 16
    choose = (lane_i[:16] == row_i[:16] + first).astype(BF16)
    by_run = lax.dot_general(
        choose, gathered, (((1,), (1,)), ((), ())), preferred_element_type=F32
    )
    for k in range(8):
        pick_z[k] = by_run[2 * k : 2 * k + 2]
    each_narrow(lambda p: to_narrow(pick_z.at[p], picks.at[z], sem_c, p))
    picks[z] = pick_z[z]

    await_all(picks.at[pl.ds(0, nz - 1)], sem_c.at[1])
    place = lax.broadcasted_iota(jnp.int32, (8, 128), 0).astype(F32)
    for h in range(2):
        await_all(slabs.at[h, pl.ds(0, nz - 1)], sem_z.at[h, 1])
        for k in range(2):
            masks = [picks[d, k : k + 1, :] == place for d in range(nz)]
            for p in range(4):
                at = 16 * p + 8 * k
                out = butterfly([slabs[h, s, at : at + 8, :] for s in range(nz)])
                for d in range(nz):
                    one = jnp.sum(jnp.where(masks[d], out[d], 0.0), axis=0, keepdims=True)
                    row = 8 * k + 4 * h + p
                    chosen[d, row : row + 1, :] = one * scale

    each_narrow(lambda p: to_narrow(chosen.at[p], back.at[z], sem_b, p))
    back[z] = chosen[z]

    lane = lane_i[:8]
    sub = row_i[:8]
    terms = []
    for d in range(nz):
        one, two = chosen[d, 0:8, :], chosen[d, 8:16, :]
        even = jnp.where(lane < 64, one, pltpu.roll(two, 64, 1))
        odd = jnp.where(lane < 64, pltpu.roll(one, 64, 1), two)
        top = jnp.where(sub < 4, even, pltpu.roll(odd, 4, 0))
        low = jnp.where(sub < 4, pltpu.roll(even, 4, 0), odd)
        terms.append(jnp.concatenate([top, low], axis=0))
    columns = jnp.concatenate(terms, axis=1)
    high = columns.astype(BF16)
    low = (columns - high.astype(F32)).astype(BF16)
    repeated = jnp.concatenate([jnp.concatenate([high, low, high], axis=1)] * 8, axis=0)
    wide_gram = lax.dot_general(
        jnp.concatenate([high, high, low], axis=1), repeated, (((1,), (1,)), ((), ())),
        preferred_element_type=F32,
    )
    diagonal = lane // 16 == sub
    for a in range(2):
        gram_own[0, a : a + 1, :] = jnp.sum(
            jnp.where(diagonal, wide_gram[8 * a : 8 * a + 8], 0.0), axis=0, keepdims=True
        )
    each_wide(lambda p: to_wide(gram_own.at[0], gram_w.at[w], sem_g.at[0], p))
    gram_w[w] = gram_own[0]

    await_all(back.at[pl.ds(0, nz - 1)], sem_b.at[1])
    for s in range(nz):
        for k in range(2):
            turn[pl.ds(2 * s + k, 8, stride=16), :] = back[s, 8 * k : 8 * k + 8, :]
    turned = turn[...].T
    ret[:, 0, :] = turned[:nw]
    ret[:, 1, :] = turned[nw:]
    each_wide(lambda p: to_wide(ret.at[p], rec.at[w], sem_p.at[pl.ds(2, 2)], p))
    rec[w] = ret[w]

    await_all(gram_w.at[pl.ds(0, nw - 1)], sem_g.at[0, 1])
    gram_zown[0] = jnp.sum(gram_w[...], axis=0)
    each_narrow(lambda p: to_narrow(gram_zown.at[0], gram_z.at[z], sem_g.at[1], p))
    gram_z[z] = gram_zown[0]

    await_all(rec.at[pl.ds(0, nw - 1)], sem_p.at[3])
    samples_ref[...] = rec[...]
    await_all(gram_z.at[pl.ds(0, nz - 1)], sem_g.at[1, 1])
    gram_ref[...] = jnp.sum(gram_z[...], axis=0) * gram_scale

    for h in range(2):
        await_all(late.at[h, pl.ds(0, nw - 1)], sem_w.at[1 + h, 0])
        await_all(slabs.at[h, pl.ds(0, nz - 1)], sem_z.at[h, 0])
    await_all(tiles.at[pl.ds(0, 8 * (nw - 1))], sem_w.at[0, 0])
    await_all(pick_tiles.at[pl.ds(0, nw - 1)], sem_p.at[0])
    await_all(rec.at[pl.ds(0, nw - 1)], sem_p.at[2])
    await_all(picks.at[pl.ds(0, nz - 1)], sem_c.at[0])
    await_all(back.at[pl.ds(0, nz - 1)], sem_b.at[0])
    await_all(gram_w.at[pl.ds(0, nw - 1)], sem_g.at[0, 0])
    await_all(gram_z.at[pl.ds(0, nz - 1)], sem_g.at[1, 0])


def arrange(samples_ref, total_ref, sketch_ref, gram_ref):
    lane = lax.broadcasted_iota(jnp.int32, (8, 128), 1)
    sub = lax.broadcasted_iota(jnp.int32, (8, 128), 0)
    group = lane // 16
    for t in range(8):
        for c in range(2):
            value = samples_ref[8 * t : 8 * t + 8, c, :]
            for bit in (1, 2, 4):
                down = pltpu.roll(pltpu.roll(value, 8 - bit, 0), 16 * bit, 1)
                up = pltpu.roll(pltpu.roll(value, bit, 0), 128 - 16 * bit, 1)
                upper, right = (sub & bit) != 0, (group & bit) != 0
                value = jnp.where(upper == right, value, jnp.where(right, down, up))
            for e in range(2):
                sketch_ref[8 * e + 4 * c : 8 * e + 4 * c + 4, 128 * t : 128 * t + 128] = value[4 * e : 4 * e + 4]

    for a in range(2):
        value = jnp.broadcast_to(total_ref[a : a + 1, :], (8, 128))
        for bit in (1, 2, 4):
            value = jnp.where((sub & bit) != 0, pltpu.roll(value, 128 - 16 * bit, 1), value)
        gram_ref[8 * a : 8 * a + 8, :] = value[:, :16]


def solution(mesh):
    nw, nz = mesh.shape["wide"], mesh.shape["narrow"]

    def shards(matrix_slab, row_signs, sample_rows):
        cols, rows = matrix_slab.shape
        samples = sample_rows.shape[0]
        dma = pltpu.SemaphoreType.DMA
        ready, total = pl.pallas_call(
            functools.partial(
                kernel, nw, nz, 1.0 / math.sqrt(rows * nw * nz), 1.0 / (samples * nw * nz)
            ),
            out_shape=(
                jax.ShapeDtypeStruct((nw, 2, 128), F32),
                jax.ShapeDtypeStruct((2, 128), F32),
            ),
            in_specs=[pl.BlockSpec(memory_space=pl.ANY)] * 3,
            out_specs=[pl.BlockSpec(memory_space=pltpu.VMEM)] * 2,
            scratch_shapes=[
                pltpu.VMEM((2, 8, 8192), F32),
                pltpu.VMEM((64, 128), jnp.int32),
                pltpu.VMEM((8, 128), jnp.int32),
                pltpu.VMEM((2, 8 * nw, 128), F32),
                pltpu.VMEM((8 * nw, 128), F32),
                pltpu.VMEM((8, 1, 128), F32),
                pltpu.VMEM((nw, 1, 128), F32),
                pltpu.VMEM((2, nz, 64, 128), F32),
                pltpu.VMEM((2, nz, 64, 128), F32),
                pltpu.VMEM((nz, 2, 128), F32),
                pltpu.VMEM((nz, 2, 128), F32),
                pltpu.VMEM((nz, 16, 128), F32),
                pltpu.VMEM((nz, 16, 128), F32),
                pltpu.VMEM((128, 128), F32),
                pltpu.VMEM((nw, 2, 128), F32),
                pltpu.VMEM((nw, 2, 128), F32),
                pltpu.VMEM((1, 2, 128), F32),
                pltpu.VMEM((nw, 2, 128), F32),
                pltpu.VMEM((1, 2, 128), F32),
                pltpu.VMEM((nz, 2, 128), F32),
                pltpu.VMEM((2, nw, 4, 128), F32),
                pltpu.VMEM((2, nw, 4, 128), F32),
                dma((4,)),
                dma((3, 2)),
                dma((2, 2)),
                dma((4,)),
                dma((2,)),
                dma((2, 2)),
                dma((2,)),
            ],
            compiler_params=pltpu.CompilerParams(collective_id=0, has_side_effects=True),
            name="hadamard_sketch",
        )(matrix_slab, row_signs.reshape(-1, 128), sample_rows.reshape(-1, 128))
        return pl.pallas_call(
            arrange,
            out_shape=(
                jax.ShapeDtypeStruct((cols, samples), F32),
                jax.ShapeDtypeStruct((cols, cols), F32),
            ),
            in_specs=[pl.BlockSpec(memory_space=pltpu.VMEM)] * 2,
            out_specs=[pl.BlockSpec(memory_space=pltpu.VMEM)] * 2,
            name="arrange",
        )(ready, total)

    in_specs = (P(None, ("wide", "narrow")), P(("wide", "narrow")), P(("wide", "narrow")))
    out_specs = (P(None, ("wide", "narrow")), P())
    return jax.shard_map(shards, mesh=mesh, in_specs=in_specs, out_specs=out_specs, check_vma=False)
```

```python
import functools
import math

import jax
import jax.numpy as jnp
from jax import lax
from jax.experimental import pallas as pl
from jax.experimental.pallas import tpu as pltpu
from jax.sharding import PartitionSpec as P

MESH = pl.DeviceIdType.MESH
F32, BF16 = jnp.float32, jnp.bfloat16


def parity_sign(a, b, bits):
    common = a & b
    parity = jnp.zeros_like(common)
    for bit in range(bits):
        parity = parity ^ (common >> bit & 1)
    return (1 - 2 * parity).astype(F32)


def butterfly(tiles):
    tiles, step = list(tiles), 1
    while step < len(tiles):
        for i in range(len(tiles)):
            if not i & step:
                a, b = tiles[i], tiles[i + step]
                tiles[i], tiles[i + step] = a + b, a - b
        step *= 2
    return tiles


def parts(value, axis):
    high = value.astype(BF16)
    low = (value - high.astype(F32)).astype(BF16)
    return jnp.concatenate([high, low], axis=axis)


def kernel(
    nw, nz, scale, gram_scale,
    x_hbm, sign_hbm, rows_hbm, samples_ref, gram_ref, x_ref, sign_ref, rows_ref,
    own, tiles, pick_own, pick_tiles, mixed, slabs, pick_z, picks,
    chosen, back, turn, ret, rec, gram_own, gram_w, gram_zown, gram_z,
    late_own, late, sem_in, sem_w, sem_z, sem_p, sem_b, sem_g, sem_c,
):
    wide, narrow = lax.axis_index("wide"), lax.axis_index("narrow")
    w, z = lax.div(wide, 8) * 8 + narrow, lax.rem(wide, 8)

    def device(group, member):
        return (lax.div(group, 8) * 8 + member, lax.rem(group, 8))

    barrier = pltpu.get_barrier_semaphore()

    inputs = [
        pltpu.make_async_copy(x_hbm.at[pl.ds(8 * h, 8)], x_ref.at[h], sem_in.at[h]) for h in range(2)
    ]
    inputs.append(pltpu.make_async_copy(sign_hbm, sign_ref, sem_in.at[2]))
    inputs.append(pltpu.make_async_copy(rows_hbm, rows_ref, sem_in.at[3]))
    for i in (0, 2, 1, 3):
        inputs[i].start()

    y, j = lax.div(w, 8), lax.rem(w, 8)

    def each_wide(body):
        def step(i, carry):
            k = lax.div(i, 8)
            half = lax.div(k + 1, 2)
            along = jnp.where(lax.rem(k, 2) == 1, 4 - half, 4 + half)
            body(lax.rem(y + along, 8) * 8 + lax.rem(j + 1 + lax.rem(i, 8), 8))
            return carry

        lax.fori_loop(0, nw - 1, step, 0)

    def each_narrow(body):
        for i in (4, 3, 5, 2, 6, 1, 7):
            body(lax.rem(z + i, nz))

    each_narrow(lambda p: pl.semaphore_signal(barrier, inc=1, device_id=device(w, p), device_id_type=MESH))
    each_wide(lambda p: pl.semaphore_signal(barrier, inc=1, device_id=device(p, z), device_id_type=MESH))

    def to_wide(src, dst, sems, p):
        pltpu.make_async_remote_copy(
            src, dst, sems.at[0], sems.at[1], device_id=device(p, z), device_id_type=MESH
        ).start()

    def to_narrow(src, dst, sems, p):
        pltpu.make_async_remote_copy(
            src, dst, sems.at[0], sems.at[1], device_id=device(w, p), device_id_type=MESH
        ).start()

    def await_all(ref, sem):
        pltpu.make_async_copy(ref, ref, sem).wait()

    lane_i = lax.broadcasted_iota(jnp.int32, (128, 128), 1)
    row_i = lax.broadcasted_iota(jnp.int32, (128, 128), 0)
    lane_table = parity_sign(lane_i, row_i, 7).astype(BF16)
    lane_table = jnp.concatenate([lane_table, lane_table], axis=0)
    def local(h):
        for g in range(8):
            part = []
            for i in range(8):
                t = g * 8 + i
                sign = sign_ref[t : t + 1, :].astype(F32)
                part.append(x_ref[h, :, 128 * t : 128 * t + 128] * sign)
            for i, tile in enumerate(butterfly(part)):
                own[h, pl.ds(8 * (g * 8 + i), 8), :] = tile
        for g in range(8):
            part = butterfly([own[h, pl.ds(8 * (i * 8 + g), 8), :] for i in range(8)])
            value = jnp.dot(
                parts(jnp.concatenate(part, axis=0), 1), lane_table, preferred_element_type=F32
            )
            for i in range(8):
                t = i * 8 + g
                if h == 0:
                    own[h, pl.ds(8 * t, 8), :] = value[8 * i : 8 * i + 8]
                    continue
                for r in range(4):
                    at = 8 * i + 2 * r
                    late_own[r & 1, t, 2 * (r >> 1) : 2 * (r >> 1) + 2, :] = value[at : at + 2]

    def send_half():
        mine = pl.ds(pl.multiple_of(w * 8, 8), 8)

        def send(p):
            to_wide(own.at[0, pl.ds(pl.multiple_of(p * 8, 8), 8)], tiles.at[mine], sem_w.at[0], p)

        each_wide(send)
        tiles[mine, :] = own[0, mine, :]

    def send_quarter(q):
        each_wide(lambda p: to_wide(late_own.at[q, p], late.at[q, w], sem_w.at[1 + q], p))
        late[q, w] = late_own[q, w]

    inputs[2].wait()
    inputs[0].wait()
    local(0)
    pl.semaphore_wait(barrier, nw - 1 + nz - 1)
    send_half()
    inputs[3].wait()
    offsets = rows_ref[...].astype(F32)
    for t in range(8):
        pick_own[t] = offsets[t : t + 1]
    each_wide(lambda p: to_wide(pick_own.at[lax.div(p, 8)], pick_tiles.at[w], sem_p, p))
    pick_tiles[w] = pick_own[lax.div(w, 8)]

    inputs[1].wait()
    local(1)
    send_quarter(0)
    send_quarter(1)

    wide_table = jnp.where(lane_i // nw == row_i // nw, parity_sign(lane_i, row_i, 6), 0.0).astype(BF16)
    wide_table = jnp.concatenate([wide_table, wide_table], axis=0)

    def mix(h, p, halves):
        value = jnp.concatenate(halves, axis=0)
        value = jnp.dot(parts(value.T, 1), wide_table, preferred_element_type=F32)
        for k in range(8):
            mixed[h, k, 16 * p : 16 * p + 16, :] = value[16 * k : 16 * k + 16]

    await_all(tiles.at[pl.ds(0, 8 * (nw - 1))], sem_w.at[0, 1])
    for p in range(4):
        mix(0, p, [tiles[pl.ds(4 * a + p, nw, stride=8), :] for a in range(2)])
    each_narrow(lambda p: to_narrow(mixed.at[0, p], slabs.at[0, z], sem_z.at[0], p))
    slabs[0, z] = mixed[0, z]
    await_all(pick_tiles.at[pl.ds(0, nw - 1)], sem_p.at[1])
    gathered = pick_tiles[...].reshape(nw, 128).astype(BF16)
    gathered = jnp.concatenate([gathered, gathered], axis=0)
    first = lax.rem(w, 8) * 16
    choose = (lane_i[:16] == row_i[:16] + first).astype(BF16)
    by_run = lax.dot_general(
        choose, gathered, (((1,), (1,)), ((), ())), preferred_element_type=F32
    )
    for k in range(8):
        pick_z[k] = by_run[2 * k : 2 * k + 2]
    each_narrow(lambda p: to_narrow(pick_z.at[p], picks.at[z], sem_c, p))
    picks[z] = pick_z[z]

    for q in range(2):
        await_all(late.at[q, pl.ds(0, nw - 1)], sem_w.at[1 + q, 1])
        for f in range(2):
            mix(1, 2 * q + f, [late[q, :, 2 * a + f, :] for a in range(2)])
        part = pl.ds(32 * q, 32)
        each_narrow(
            lambda p: to_narrow(mixed.at[1, p, part], slabs.at[1, z, part], sem_z.at[1], p)
        )
    slabs[1, z] = mixed[1, z]

    await_all(picks.at[pl.ds(0, nz - 1)], sem_c.at[1])
    place = lax.broadcasted_iota(jnp.int32, (8, 128), 0).astype(F32)
    for h in range(2):
        await_all(slabs.at[h, pl.ds(0, nz - 1)], sem_z.at[h, 1])
        for k in range(2):
            masks = [picks[d, k : k + 1, :] == place for d in range(nz)]
            for p in range(4):
                at = 16 * p + 8 * k
                out = butterfly([slabs[h, s, at : at + 8, :] for s in range(nz)])
                for d in range(nz):
                    one = jnp.sum(jnp.where(masks[d], out[d], 0.0), axis=0, keepdims=True)
                    row = 8 * k + 4 * h + p
                    chosen[d, row : row + 1, :] = one * scale

    each_narrow(lambda p: to_narrow(chosen.at[p], back.at[z], sem_b, p))
    back[z] = chosen[z]

    lane = lane_i[:8]
    sub = row_i[:8]
    terms = []
    for d in range(nz):
        one, two = chosen[d, 0:8, :], chosen[d, 8:16, :]
        even = jnp.where(lane < 64, one, pltpu.roll(two, 64, 1))
        odd = jnp.where(lane < 64, pltpu.roll(one, 64, 1), two)
        top = jnp.where(sub < 4, even, pltpu.roll(odd, 4, 0))
        low = jnp.where(sub < 4, pltpu.roll(even, 4, 0), odd)
        terms.append(jnp.concatenate([top, low], axis=0))
    columns = jnp.concatenate(terms, axis=1)
    high = columns.astype(BF16)
    low = (columns - high.astype(F32)).astype(BF16)
    repeated = jnp.concatenate([jnp.concatenate([high, low, high], axis=1)] * 8, axis=0)
    wide_gram = lax.dot_general(
        jnp.concatenate([high, high, low], axis=1), repeated, (((1,), (1,)), ((), ())),
        preferred_element_type=F32,
    )
    diagonal = lane // 16 == sub
    for a in range(2):
        gram_own[0, a : a + 1, :] = jnp.sum(
            jnp.where(diagonal, wide_gram[8 * a : 8 * a + 8], 0.0), axis=0, keepdims=True
        )
    each_wide(lambda p: to_wide(gram_own.at[0], gram_w.at[w], sem_g.at[0], p))
    gram_w[w] = gram_own[0]

    await_all(back.at[pl.ds(0, nz - 1)], sem_b.at[1])
    for s in range(nz):
        for k in range(2):
            turn[pl.ds(2 * s + k, 8, stride=16), :] = back[s, 8 * k : 8 * k + 8, :]
    turned = turn[...].T
    ret[:, 0, :] = turned[:nw]
    ret[:, 1, :] = turned[nw:]
    each_wide(lambda p: to_wide(ret.at[p], rec.at[w], sem_p.at[pl.ds(2, 2)], p))
    rec[w] = ret[w]

    await_all(gram_w.at[pl.ds(0, nw - 1)], sem_g.at[0, 1])
    gram_zown[0] = jnp.sum(gram_w[...], axis=0)
    each_narrow(lambda p: to_narrow(gram_zown.at[0], gram_z.at[z], sem_g.at[1], p))
    gram_z[z] = gram_zown[0]

    await_all(rec.at[pl.ds(0, nw - 1)], sem_p.at[3])
    samples_ref[...] = rec[...]
    await_all(gram_z.at[pl.ds(0, nz - 1)], sem_g.at[1, 1])
    gram_ref[...] = jnp.sum(gram_z[...], axis=0) * gram_scale

    for h in range(2):
        await_all(late.at[h, pl.ds(0, nw - 1)], sem_w.at[1 + h, 0])
        await_all(slabs.at[h, pl.ds(0, nz - 1)], sem_z.at[h, 0])
    await_all(tiles.at[pl.ds(0, 8 * (nw - 1))], sem_w.at[0, 0])
    await_all(pick_tiles.at[pl.ds(0, nw - 1)], sem_p.at[0])
    await_all(rec.at[pl.ds(0, nw - 1)], sem_p.at[2])
    await_all(picks.at[pl.ds(0, nz - 1)], sem_c.at[0])
    await_all(back.at[pl.ds(0, nz - 1)], sem_b.at[0])
    await_all(gram_w.at[pl.ds(0, nw - 1)], sem_g.at[0, 0])
    await_all(gram_z.at[pl.ds(0, nz - 1)], sem_g.at[1, 0])


def arrange(samples_ref, total_ref, sketch_ref, gram_ref):
    lane = lax.broadcasted_iota(jnp.int32, (8, 128), 1)
    sub = lax.broadcasted_iota(jnp.int32, (8, 128), 0)
    group = lane // 16
    for t in range(8):
        for c in range(2):
            value = samples_ref[8 * t : 8 * t + 8, c, :]
            for bit in (1, 2, 4):
                down = pltpu.roll(pltpu.roll(value, 8 - bit, 0), 16 * bit, 1)
                up = pltpu.roll(pltpu.roll(value, bit, 0), 128 - 16 * bit, 1)
                upper, right = (sub & bit) != 0, (group & bit) != 0
                value = jnp.where(upper == right, value, jnp.where(right, down, up))
            for e in range(2):
                sketch_ref[8 * e + 4 * c : 8 * e + 4 * c + 4, 128 * t : 128 * t + 128] = value[4 * e : 4 * e + 4]

    for a in range(2):
        value = jnp.broadcast_to(total_ref[a : a + 1, :], (8, 128))
        for bit in (1, 2, 4):
            value = jnp.where((sub & bit) != 0, pltpu.roll(value, 128 - 16 * bit, 1), value)
        gram_ref[8 * a : 8 * a + 8, :] = value[:, :16]


def solution(mesh):
    nw, nz = mesh.shape["wide"], mesh.shape["narrow"]

    def shards(matrix_slab, row_signs, sample_rows):
        cols, rows = matrix_slab.shape
        samples = sample_rows.shape[0]
        dma = pltpu.SemaphoreType.DMA
        ready, total = pl.pallas_call(
            functools.partial(
                kernel, nw, nz, 1.0 / math.sqrt(rows * nw * nz), 1.0 / (samples * nw * nz)
            ),
            out_shape=(
                jax.ShapeDtypeStruct((nw, 2, 128), F32),
                jax.ShapeDtypeStruct((2, 128), F32),
            ),
            in_specs=[pl.BlockSpec(memory_space=pl.ANY)] * 3,
            out_specs=[pl.BlockSpec(memory_space=pltpu.VMEM)] * 2,
            scratch_shapes=[
                pltpu.VMEM((2, 8, 8192), F32),
                pltpu.VMEM((64, 128), jnp.int32),
                pltpu.VMEM((8, 128), jnp.int32),
                pltpu.VMEM((2, 8 * nw, 128), F32),
                pltpu.VMEM((8 * nw, 128), F32),
                pltpu.VMEM((8, 1, 128), F32),
                pltpu.VMEM((nw, 1, 128), F32),
                pltpu.VMEM((2, nz, 64, 128), F32),
                pltpu.VMEM((2, nz, 64, 128), F32),
                pltpu.VMEM((nz, 2, 128), F32),
                pltpu.VMEM((nz, 2, 128), F32),
                pltpu.VMEM((nz, 16, 128), F32),
                pltpu.VMEM((nz, 16, 128), F32),
                pltpu.VMEM((128, 128), F32),
                pltpu.VMEM((nw, 2, 128), F32),
                pltpu.VMEM((nw, 2, 128), F32),
                pltpu.VMEM((1, 2, 128), F32),
                pltpu.VMEM((nw, 2, 128), F32),
                pltpu.VMEM((1, 2, 128), F32),
                pltpu.VMEM((nz, 2, 128), F32),
                pltpu.VMEM((2, nw, 4, 128), F32),
                pltpu.VMEM((2, nw, 4, 128), F32),
                dma((4,)),
                dma((3, 2)),
                dma((2, 2)),
                dma((4,)),
                dma((2,)),
                dma((2, 2)),
                dma((2,)),
            ],
            compiler_params=pltpu.CompilerParams(collective_id=0, has_side_effects=True),
            name="hadamard_sketch",
        )(matrix_slab, row_signs.reshape(-1, 128), sample_rows.reshape(-1, 128))
        return pl.pallas_call(
            arrange,
            out_shape=(
                jax.ShapeDtypeStruct((cols, samples), F32),
                jax.ShapeDtypeStruct((cols, cols), F32),
            ),
            in_specs=[pl.BlockSpec(memory_space=pltpu.VMEM)] * 2,
            out_specs=[pl.BlockSpec(memory_space=pltpu.VMEM)] * 2,
            name="arrange",
        )(ready, total)

    in_specs = (P(None, ("wide", "narrow")), P(("wide", "narrow")), P(("wide", "narrow")))
    out_specs = (P(None, ("wide", "narrow")), P())
    return jax.shard_map(shards, mesh=mesh, in_specs=in_specs, out_specs=out_specs, check_vma=False)
```
